32 devices in a mesh: batch: 4 (over x, core), cache: 8 (over z, y).
Axes of the slice: x: 2, y: 2, z: 4, core: 2. Of those that a mesh axis runs over, the one named last changes fastest.
Arguments:
- arrivals: bfloat16 [16, 4, 4096], P('batch', None, 'cache'), may hold values from -6 to 6
- norm_gain: float32 [4096], replicated, may hold values from 0.25 to 1.75
- qkv_weight: bfloat16 [4096, 6144], P(None, 'cache'), may hold values from -0.09375 to 0.09375
- out_weight: bfloat16 [4096, 4096], P('cache'), may hold values from -0.09375 to 0.09375
- kv_cache: bfloat16 [16, 16, 2, 8, 128, 128], P('batch', 'cache'), as said below
- slot: int32 [16], replicated, may hold values from 0 to 15, each once
- positions: int32 [16], P('batch'), may hold values from 1664 to 2044
- tile_lists: int32 [16, 8], P('batch'), may hold values from 0 to 15, as said below
Outputs:
- attended: bfloat16 [16, 4, 4096], P('batch', None, 'cache')
The draws below stay inside these ranges and needn't reach their ends.
Inputs may be any that keep to these rules, and one draw needn't show every extreme that they name: `tile_lists`: tiles of a row are distinct; the first is the tile of position positions - 1, the others lie at most 12 tiles before it. `kv_cache`: entries are of magnitude at most 240.
All inputs are finite; a program needn't handle non-finite values.
Results may differ from the reference program's by a relative error of at most 0.022.
Values may be sent and summed in bfloat16 or wider, within the bound.
A program may use at most 64 MiB of HBM per device.

```python
import math
import jax
import jax.numpy as jnp
from jax import lax

D = 4096
HEADS = 32
KVH = 8
HD = 128
TILE = 128
STEPS = 4
WIN = 8
NEAR = 12
IMW = 64
CW = 16
REQS = 16
TILES = 16


def request_plan(key):
    first_key, second_key = jax.random.split(jax.random.fold_in(key, 7))
    lowest = (NEAR + 1) * TILE
    highest = TILES * TILE - STEPS
    position = jax.random.randint(first_key, (REQS,), lowest, highest + 1, dtype=jnp.int32)
    position = position.at[0].set(highest).at[1].set(lowest)
    current = (position - 1) // TILE
    row_keys = jax.random.split(second_key, REQS)
    shuffled = jax.vmap(lambda row_key: jax.random.permutation(row_key, NEAR))(row_keys)[:, :WIN - 1].astype(jnp.int32)
    farthest = (NEAR - 1 - jnp.arange(WIN - 1, dtype=jnp.int32)).astype(jnp.int32)
    shuffled = shuffled.at[1].set(farthest)
    listing = jnp.concatenate([current[:, None], current[:, None] - 1 - shuffled], axis=1)
    return (position.astype(jnp.int32), listing.astype(jnp.int32))


def draw_positions(key, part):
    return request_plan(key)[0]


def draw_tile_lists(key, part):
    return request_plan(key)[1]


def draw_kv_cache(key, part):
    base_key = jax.random.fold_in(jax.random.fold_in(key, 11), 0)
    values = jnp.clip(jax.random.normal(base_key, (REQS, TILES, 2, KVH, TILE, HD), jnp.float32), -6.0, 6.0)
    return values.astype(jnp.bfloat16)


def block_levels(stream_key, dims, cuts, least, largest):
    gain, own = 1.0, jax.random.fold_in(stream_key, 6)
    for dim, parts in cuts:
        draws = jnp.exp(jax.random.uniform(jax.random.fold_in(own, dim), (parts,), jnp.float32, least / len(cuts), largest / len(cuts)))
        gain = gain * jnp.repeat(draws, dims[dim] // parts).reshape([-1 if axis == dim else 1 for axis in range(len(dims))])
    return gain


def normal_values(own_key, shape, spread, limit, cuts=(), held_as=jnp.bfloat16):
    values = jax.random.normal(own_key, shape, jnp.float32) * spread
    if len(cuts) > 0:
        values = block_levels(own_key, shape, cuts, -0.22, 0.18) * values
    return jnp.clip(values, min=-limit, max=limit).astype(held_as)


def setup_inputs(seed: int = 0) -> dict:
    keys = jax.random.split(jax.random.key(seed), 9)
    return {
        "arrivals": normal_values(keys[0], (REQS, STEPS, D), 1.0, 6.0, ((0, 4), (2, 8))),
        "norm_gain": jnp.clip(1.0 + 0.15 * jax.random.normal(keys[1], (D,), jnp.float32), 0.25, 1.75),
        "qkv_weight": normal_values(keys[2], (D, KVH * (HEADS // KVH + 2) * HD), D ** -0.5, 0.09375, ((1, 8),)),
        "out_weight": normal_values(keys[3], (HEADS * HD, D), (HEADS * HD) ** -0.5, 0.09375, ((0, 8),)),
        "kv_cache": draw_kv_cache(jax.random.fold_in(keys[8], 71), 0),
        "slot": jax.random.permutation(keys[5], REQS).astype(jnp.int32),
        "positions": draw_positions(jax.random.fold_in(keys[8], 71), 0),
        "tile_lists": draw_tile_lists(jax.random.fold_in(keys[8], 71), 0),
    }


epsilon = 1e-05

def window_mask(query_pos, key_pos):
    return jnp.abs(key_pos % IMW - query_pos % IMW) <= CW

def reference(arrivals, norm_gain, qkv_weight, out_weight, kv_cache, slot, positions, tile_lists):
    groups = HEADS // KVH
    inverse = jnp.argsort(slot).astype(jnp.int32)
    ordered = jnp.take(arrivals, inverse, axis=0).astype(jnp.float32)
    normed = (ordered * lax.rsqrt(lax.optimization_barrier(jnp.mean(ordered * ordered, axis=-1, keepdims=True)) + epsilon) * norm_gain).astype(jnp.bfloat16)
    projected = jnp.dot(normed.reshape(REQS * STEPS, D), qkv_weight, preferred_element_type=jnp.float32)
    projected = projected.astype(jnp.bfloat16).reshape(REQS, STEPS, KVH, groups + 2, HD)
    score_scale = 1.0 / math.sqrt(HD)
    step_index = jnp.arange(STEPS, dtype=jnp.int32)

    def one_request(inputs):
        heads_row, cache_row, position, listing = inputs
        queries = heads_row[:, :, :groups].astype(jnp.float32)
        new_keys = heads_row[:, :, groups].astype(jnp.float32)
        new_vals = heads_row[:, :, groups + 1].astype(jnp.float32)
        chosen = jnp.take(cache_row, listing.astype(jnp.int32), axis=0).astype(jnp.float32)
        key_pos = listing[:, None] * TILE + jnp.arange(TILE, dtype=jnp.int32)[None, :]
        query_pos = position + step_index
        key_valid = (key_pos[None] < position) & window_mask(query_pos[:, None, None], key_pos[None])
        scores = jnp.einsum('sjgd,wjkd->jgswk', queries, chosen[:, 0]) * score_scale
        new_scores = jnp.einsum('sjgd,ujd->jgsu', queries, new_keys) * score_scale
        new_valid = (step_index[:, None] >= step_index[None, :]) & window_mask(query_pos[:, None], query_pos[None, :])
        top_score = jnp.maximum(lax.optimization_barrier(jnp.max(jnp.where(key_valid, scores, -jnp.inf), axis=(-2, -1))), lax.optimization_barrier(jnp.max(jnp.where(new_valid, new_scores, -jnp.inf), axis=-1)))
        weights = jnp.where(key_valid, jnp.exp(scores - top_score[..., None, None]), 0.0)
        new_weights = jnp.where(new_valid, jnp.exp(new_scores - top_score[..., None]), 0.0)
        totals = lax.optimization_barrier(jnp.sum(weights, axis=(-2, -1))) + lax.optimization_barrier(jnp.sum(new_weights, axis=-1))
        numerator = jnp.einsum('jgswk,wjkd->jgsd', weights.astype(jnp.bfloat16).astype(jnp.float32), chosen[:, 1])
        numerator = numerator + jnp.einsum('jgsu,ujd->jgsd', new_weights.astype(jnp.bfloat16).astype(jnp.float32), new_vals)
        attention = (numerator / totals[..., None]).astype(jnp.bfloat16)
        return attention.transpose(2, 0, 1, 3).reshape(STEPS, HEADS * HD)
    attention = lax.map(one_request, (projected, kv_cache, positions, tile_lists))
    attended = jnp.dot(attention.reshape(REQS * STEPS, HEADS * HD), out_weight, preferred_element_type=jnp.float32)
    return attended.astype(jnp.bfloat16).reshape(REQS, STEPS, D)
```

```python
import functools
import math

import jax
import jax.numpy as jnp
from jax import lax
from jax.experimental import pallas as pl
from jax.experimental.pallas import tpu as pltpu
from jax.sharding import PartitionSpec as P

HEADS = 32
KVH = 8
HD = 128
TILE = 128
IMW = 64
CW = 16


epsilon = 1e-05
very_low = -1e30


VMEM = pl.BlockSpec(memory_space=pltpu.VMEM)
MESH = pl.DeviceIdType.MESH


def greet(axis, size, me):
    barrier = pltpu.get_barrier_semaphore()
    for step in range(1, size):
        pl.semaphore_signal(
            barrier, inc=1, device_id={axis: lax.rem(me + step, size)}, device_id_type=MESH
        )
    pl.semaphore_wait(barrier, size - 1)


def send(source, target, send_sem, recv_sem, axis, peer):
    copy = pltpu.make_async_remote_copy(
        src_ref=source,
        dst_ref=target,
        send_sem=send_sem,
        recv_sem=recv_sem,
        device_id={axis: peer},
        device_id_type=MESH,
    )
    copy.start()
    return copy


def columns_of(index, width):
    return pl.ds(pl.multiple_of(index * width, width), width)


def communicate(kernel, out_shape, scratch, collective_id, *arrays):
    count = len(out_shape) if isinstance(out_shape, tuple) else 0
    return pl.pallas_call(
        kernel,
        out_shape=out_shape,
        in_specs=[VMEM] * len(arrays),
        out_specs=(VMEM,) * count if count else VMEM,
        scratch_shapes=scratch,
        compiler_params=pltpu.CompilerParams(collective_id=collective_id, has_side_effects=True),
    )(*arrays)


def gather_kernel(axis, size, on_columns, x_ref, out_ref, send_sems, recv_sems, own_sem):
    me = lax.axis_index(axis)
    if on_columns:
        mine = out_ref.at[:, columns_of(me, x_ref.shape[1])]
    else:
        mine = out_ref.at[me]
    own = pltpu.make_async_copy(x_ref, mine, own_sem)
    own.start()
    greet(axis, size, me)
    copies = [
        send(x_ref, mine, send_sems.at[k], recv_sems.at[k], axis, lax.rem(me + k, size))
        for k in range(1, size)
    ]
    own.wait()
    for copy in copies:
        copy.wait()


def gather(block, axis, size, on_columns, collective_id):
    rows, width = block.shape
    shape = (rows, size * width) if on_columns else (size, rows, width)
    return communicate(
        functools.partial(gather_kernel, axis, size, on_columns),
        jax.ShapeDtypeStruct(shape, block.dtype),
        [
            pltpu.SemaphoreType.DMA((size,)),
            pltpu.SemaphoreType.DMA((size,)),
            pltpu.SemaphoreType.DMA,
        ],
        collective_id,
        block,
    )


def swap_kernel(axis, size, a_ref, b_ref, a_out, b_out, send_sems, recv_sems, own_sems):
    me = lax.axis_index(axis)
    pairs = ((a_ref, a_out), (b_ref, b_out))
    owns = []
    for index, (source, target) in enumerate(pairs):
        own = pltpu.make_async_copy(source.at[me], target.at[me], own_sems.at[index])
        own.start()
        owns.append(own)
    greet(axis, size, me)
    copies = []
    for k in range(1, size):
        peer = lax.rem(me + k, size)
        for index, (source, target) in enumerate(pairs):
            copies.append(
                send(
                    source.at[peer],
                    target.at[me],
                    send_sems.at[index, k],
                    recv_sems.at[index, k],
                    axis,
                    peer,
                )
            )
    for copy in owns + copies:
        copy.wait()


def swap(a, b, axis, size, collective_id):
    return communicate(
        functools.partial(swap_kernel, axis, size),
        (jax.ShapeDtypeStruct(a.shape, a.dtype), jax.ShapeDtypeStruct(b.shape, b.dtype)),
        [
            pltpu.SemaphoreType.DMA((2, size)),
            pltpu.SemaphoreType.DMA((2, size)),
            pltpu.SemaphoreType.DMA((2,)),
        ],
        collective_id,
        a,
        b,
    )


def scatter_kernel(axis, size, x_ref, out_ref, held, send_sems, recv_sems):
    me = lax.axis_index(axis)
    width = out_ref.shape[1]
    greet(axis, size, me)
    copies = []
    for k in range(1, size):
        peer = lax.rem(me + k, size)
        copies.append(
            send(
                x_ref.at[:, columns_of(peer, width)],
                held.at[k],
                send_sems.at[k],
                recv_sems.at[k],
                axis,
                peer,
            )
        )
    total = x_ref[:, columns_of(me, width)].astype(jnp.float32)
    for k in range(1, size):
        copies[k - 1].wait_recv()
        total = total + held[k].astype(jnp.float32)
    out_ref[...] = total.astype(out_ref.dtype)
    for copy in copies:
        copy.wait_send()


def reduce_scatter(partial, axis, size, collective_id):
    rows, width = partial.shape[0], partial.shape[1] // size
    return communicate(
        functools.partial(scatter_kernel, axis, size),
        jax.ShapeDtypeStruct((rows, width), partial.dtype),
        [
            pltpu.VMEM((size, rows, width), partial.dtype),
            pltpu.SemaphoreType.DMA((size,)),
            pltpu.SemaphoreType.DMA((size,)),
        ],
        collective_id,
        partial,
    )


def window_mask(query_pos, key_pos):
    return jnp.abs(key_pos % IMW - query_pos % IMW) <= CW


def shards(batch_size, cache_size, arrivals, norm_gain, qkv_weight, out_weight, kv_cache, slot, positions, tile_lists):
    row_count = positions.shape[0]
    step_count = arrivals.shape[1]
    groups = HEADS // KVH
    head_share = out_weight.shape[0] // HD
    head_start = lax.axis_index("cache") * head_share
    everyone = gather(
        arrivals.reshape(row_count * step_count, -1), "batch", batch_size, False, 0
    ).reshape(batch_size * row_count * step_count, -1)
    my_row = lax.axis_index("batch") * row_count + jnp.arange(row_count * step_count) // step_count
    my_step = jnp.arange(row_count * step_count) % step_count
    their_row = jnp.repeat(slot, step_count)
    their_step = jnp.arange(slot.shape[0] * step_count) % step_count
    chosen = (my_row[:, None] == their_row[None]) & (my_step[:, None] == their_step[None])
    picked = jnp.dot(
        chosen.astype(jnp.bfloat16), everyone, preferred_element_type=jnp.float32
    ).astype(jnp.bfloat16)
    whole = gather(picked, "cache", cache_size, True, 1)
    wide_values = whole.astype(jnp.float32)
    normed = (
        wide_values
        * lax.rsqrt(jnp.mean(wide_values * wide_values, axis=-1, keepdims=True) + epsilon)
        * norm_gain
    ).astype(jnp.bfloat16)
    projected = jnp.dot(normed, qkv_weight, preferred_element_type=jnp.float32)
    heads_all = gather(projected.astype(jnp.bfloat16), "cache", cache_size, True, 2).reshape(
        row_count, step_count, KVH, groups + 2, HD
    )
    queries = heads_all[:, :, :, :groups, :]
    new_keys = heads_all[:, :, :, groups, :]
    new_vals = heads_all[:, :, :, groups + 1, :]
    score_scale = 1.0 / math.sqrt(HD)
    tiles_here = kv_cache.shape[1]
    tile_ids = lax.axis_index("cache") * tiles_here + jnp.arange(tiles_here, dtype=jnp.int32)
    listed = jnp.any(tile_lists[:, :, None] == tile_ids[None, None, :], axis=1)
    key_pos = tile_ids[:, None] * TILE + jnp.arange(TILE, dtype=jnp.int32)[None, :]
    step_index = jnp.arange(step_count, dtype=jnp.int32)
    query_pos = positions[:, None] + step_index[None, :]
    key_valid = listed[:, None, :, None] & (key_pos[None, None] < positions[:, None, None, None])
    key_valid = key_valid & window_mask(query_pos[:, :, None, None], key_pos[None, None])
    valid_wide = key_valid[:, None, None]
    scores = (
        jnp.einsum(
            "bsjgd,btjkd->bjgstk", queries, kv_cache[:, :, 0], preferred_element_type=jnp.float32
        )
        * score_scale
    )
    new_valid = (step_index[None, :, None] >= step_index[None, None, :]) & window_mask(
        query_pos[:, :, None], query_pos[:, None, :]
    )
    new_scores = (
        jnp.einsum("bsjgd,bujd->bjgsu", queries, new_keys, preferred_element_type=jnp.float32)
        * score_scale
    )
    new_max = jnp.max(jnp.where(new_valid[:, None, None], new_scores, -jnp.inf), axis=-1)
    local_max = jnp.max(jnp.where(valid_wide, scores, very_low), axis=(-2, -1))
    values_here = kv_cache[:, :, 1]

    def own_heads(array):
        merged = array.reshape((row_count, HEADS) + array.shape[3:])
        return lax.dynamic_slice_in_dim(merged, head_start, head_share, 1)

    weights = jnp.where(valid_wide, jnp.exp(scores - local_max[..., None, None]), 0.0)
    totals = jnp.sum(weights, axis=(-2, -1))
    numerator = jnp.einsum(
        "bjgstk,btjkd->bjgsd",
        weights.astype(jnp.bfloat16),
        values_here,
        preferred_element_type=jnp.float32,
    )
    entries = row_count * head_share * step_count

    def by_holder(array):
        split = array.reshape((row_count, cache_size, head_share, step_count) + array.shape[4:])
        return jnp.moveaxis(split, 1, 0)

    sums_out = by_holder(numerator.astype(jnp.bfloat16)).reshape(cache_size, entries, HD)
    stats_out = jnp.stack(
        [by_holder(array).reshape(cache_size, entries) for array in (totals, local_max)], axis=1
    )
    stats_out = jnp.pad(stats_out, ((0, 0), (0, 6), (0, -entries % 128)))
    part_sums, part_stats = swap(sums_out, stats_out, "cache", cache_size, 3)
    kept = (cache_size, row_count, head_share, step_count)
    part_sums = part_sums.reshape(kept + (HD,)).astype(jnp.float32)
    part_totals = part_stats[:, 0, :entries].reshape(kept)
    part_peaks = part_stats[:, 1, :entries].reshape(kept)
    top_own = jnp.maximum(jnp.max(part_peaks, axis=0), own_heads(new_max))
    factor = jnp.exp(part_peaks - top_own[None])
    numer_own = jnp.sum(part_sums * factor[..., None], axis=0)
    total_own = jnp.sum(part_totals * factor, axis=0)
    own_new = own_heads(new_scores)
    new_weights = jnp.where(new_valid[:, None], jnp.exp(own_new - top_own[..., None]), 0.0)
    own_vals = lax.dynamic_slice_in_dim(
        jnp.repeat(new_vals, groups, axis=2), head_start, head_share, 2
    )
    total_all = total_own + jnp.sum(new_weights, axis=-1)
    numer_all = numer_own + jnp.einsum(
        "bhsu,buhd->bhsd",
        new_weights.astype(jnp.bfloat16),
        own_vals,
        preferred_element_type=jnp.float32,
    )
    attention = (numer_all / total_all[..., None]).astype(jnp.bfloat16)
    attn_flat = attention.transpose(0, 2, 1, 3).reshape(row_count * step_count, head_share * HD)
    partial_out = jnp.dot(attn_flat, out_weight, preferred_element_type=jnp.float32)
    return reduce_scatter(partial_out.astype(jnp.bfloat16), "cache", cache_size, 4).reshape(
        row_count, step_count, -1
    )


def solution(mesh):
    in_specs = (
        P("batch", None, "cache"),
        P(),
        P(None, "cache"),
        P("cache", None),
        P("batch", "cache", None, None, None, None),
        P(),
        P("batch"),
        P("batch", None),
    )
    out_specs = P("batch", None, "cache")
    body = functools.partial(shards, mesh.shape["batch"], mesh.shape["cache"])
    return jax.shard_map(body, mesh=mesh, in_specs=in_specs, out_specs=out_specs, check_vma=False)
```
